32 devices in a mesh: groups: 2 (over y), ctx: 4 (over z), heads: 2 (over x), rep: 2 (over core).
Axes of the slice: x: 2, y: 2, z: 4, core: 2. Of those that a mesh axis runs over, the one named last changes fastest.
Arguments:
- queries: bfloat16 [24576, 32, 128], P(('groups', 'ctx'), ('heads', 'rep')), parts along dimension 0, may hold values from -14 to 14
- keys: bfloat16 [24576, 8, 128], P(('groups', 'ctx'), 'heads'), parts along dimension 0, may hold values from -14 to 14
- values: bfloat16 [24576, 8, 128], P(('groups', 'ctx'), 'heads'), parts along dimension 0, may hold values from -6 to 6
- chosen: int32 [8, 192, 8], P('heads', ('groups', 'ctx')), parts along dimension 1, may hold values from 0 to 95, as said below
Outputs:
- attended: bfloat16 [24576, 32, 128], P(('groups', 'ctx'), ('heads', 'rep')), parts along dimension 0
The draws below stay inside these ranges and needn't reach their ends.
There are 2 independent parts, one for each index of `groups`. The reference program is written for one: setup_inputs(seed, part) draws one part's arguments, and reference() takes and returns one part's arrays. A program takes and returns all parts, laid end to end along the dimension named above; each array names one. Nothing has to cross between parts.
Inputs may be any that keep to these rules, and one draw needn't show every extreme that they name: chosen[h, b, 0] = b. The other entries of a list are at most b and differ from each other, except that b itself may be repeated. For one key-value head, the 24 query blocks of one sequence shard list at most 2 distinct blocks of any other shard.
All inputs are finite; a program needn't handle non-finite values.
Results may differ from the reference program's by a relative error of at most 0.0046.
Values may be sent and summed in bfloat16 or wider, within the bound.
A program may use at most 128 MiB of HBM per device.

```python
import jax
import jax.numpy as jnp
from jax import lax

QUERY_HEADS = 32
KEY_VALUE_HEADS = 8
HEAD_SIZE = 128
TOPK = 8
REMOTE_BLOCK_MAX = 2
QB_DEV = 24
CTX_SHARDS = 4
SEQUENCE_TOKENS = 12288


def pair_draw(key):
    pair_key = jax.random.fold_in(key, 7)
    key_seed_first, key_two = jax.random.split(pair_key, 2)
    key_pattern = jnp.clip(jax.random.normal(key_seed_first, (SEQUENCE_TOKENS, KEY_VALUE_HEADS, HEAD_SIZE), jnp.float32), -4.0, 4.0)
    query_field = jnp.clip(jax.random.normal(key_two, (SEQUENCE_TOKENS, QUERY_HEADS, HEAD_SIZE), jnp.float32), -4.0, 4.0)
    return (query_field, key_pattern)


def draw_queries(key, part):
    return pair_draw(key)[0].astype(jnp.bfloat16)


def draw_keys(key, part):
    return pair_draw(key)[1].astype(jnp.bfloat16)


def draw_chosen(key, part):
    shard_count = CTX_SHARDS
    blocks_per_shard = QB_DEV
    block_count = shard_count * blocks_per_shard
    leading_key, following_key = jax.random.split(jax.random.fold_in(key, 11))
    unscaled_scores = jax.random.randint(leading_key, (KEY_VALUE_HEADS, shard_count, shard_count, blocks_per_shard), 0, 1 << 20) * blocks_per_shard + jnp.arange(blocks_per_shard, dtype=jnp.int32)
    unused_score, selected_resident = lax.top_k(unscaled_scores, REMOTE_BLOCK_MAX)
    source_offset = (jnp.arange(shard_count, dtype=jnp.int32) * blocks_per_shard)[None, None, :, None]
    remote_blocks = (source_offset + selected_resident).reshape(KEY_VALUE_HEADS, shard_count, shard_count * REMOTE_BLOCK_MAX)
    block_numbers = jnp.arange(block_count, dtype=jnp.int32)
    device_of = block_numbers // blocks_per_shard
    within = block_numbers % blocks_per_shard
    remote_rows = jnp.repeat(remote_blocks, blocks_per_shard, axis=1)
    resident_rows = device_of[:, None] * blocks_per_shard + jnp.arange(blocks_per_shard, dtype=jnp.int32)[None, :]
    resident_rows = jnp.broadcast_to(resident_rows[None], (KEY_VALUE_HEADS, block_count, blocks_per_shard))
    candidates = jnp.concatenate([remote_rows, resident_rows], axis=-1)
    full_width = shard_count * REMOTE_BLOCK_MAX + blocks_per_shard
    slot_table = jnp.arange(full_width, dtype=jnp.int32)
    remote_valid = jnp.arange(shard_count * REMOTE_BLOCK_MAX, dtype=jnp.int32)[None, :] // REMOTE_BLOCK_MAX < device_of[:, None]
    local_valid = jnp.arange(blocks_per_shard, dtype=jnp.int32)[None, :] < within[:, None]
    valid = jnp.concatenate([remote_valid, local_valid], axis=-1)[None]
    full_scores = jax.random.randint(following_key, (KEY_VALUE_HEADS, block_count, full_width), 0, 1 << 20) * full_width + slot_table
    live_count = jnp.maximum(device_of * REMOTE_BLOCK_MAX, 1)[:, None]
    forced = jnp.zeros((block_count, full_width), dtype=bool)
    for turn in range(3):
        forced = forced | (slot_table[None, :] == (within[:, None] + turn * blocks_per_shard) % live_count)
    forced = forced & (device_of[:, None] >= 1)
    full_scores = jnp.where(forced[None], (1 << 20) * full_width + full_width + slot_table, full_scores)
    full_scores = jnp.where(valid, full_scores, -1 - slot_table)
    best_score, best_index = lax.top_k(full_scores, TOPK - 1)
    picked = jnp.take_along_axis(candidates, best_index, axis=-1)
    picked = jnp.where(best_score >= 0, picked, block_numbers[None, :, None])
    own_device = jnp.broadcast_to(block_numbers[None, :, None], (KEY_VALUE_HEADS, block_count, 1))
    return jnp.concatenate([own_device, picked], axis=-1).astype(jnp.int32)


def steps_of(own_key, extent, cuts, least, largest):
    gain = 1.0
    for position, parts in cuts:
        draws = jax.random.uniform(jax.random.fold_in(jax.random.fold_in(own_key, 6), position), (parts,), jnp.float32, least / len(cuts), largest / len(cuts))
        gain = gain * jnp.repeat(jnp.exp(draws), extent[position] // parts).reshape((-1,) + (1,) * (len(extent) - 1 - position))
    return gain


def centred(own_key, shape, deviation, reach, shards=(), kind=jnp.bfloat16):
    factor_of = steps_of(own_key, shape, shards, -0.22, 0.18) if shards else 1.0
    drawn = jax.random.normal(own_key, shape, jnp.float32) * deviation * factor_of
    return jnp.minimum(jnp.maximum(drawn, -reach), reach).astype(kind)


def setup_inputs(seed: int = 0, part: int = 0) -> dict:
    key_of = jax.random.split(jax.random.key(seed), 5)
    part_keys = jax.random.split(jax.random.fold_in(key_of[4], part), 5)
    return {
        "queries": draw_queries(jax.random.fold_in(jax.random.fold_in(key_of[4], part), 71), part),
        "keys": draw_keys(jax.random.fold_in(jax.random.fold_in(key_of[4], part), 71), part),
        "values": centred(part_keys[2], (SEQUENCE_TOKENS, KEY_VALUE_HEADS, HEAD_SIZE), 1.0, 6.0, ((0, 4), (1, 2))),
        "chosen": draw_chosen(jax.random.fold_in(jax.random.fold_in(key_of[4], part), 71), part),
    }


def attend(query_part, key_part, value_part, chosen_part):
    block_len = query_part.shape[1]
    head_dim = query_part.shape[-1]
    picks = chosen_part.shape[-1]
    scores = jnp.einsum("gqeah,egkh->egaqk", query_part.astype(jnp.float32), key_part.astype(jnp.float32)) * (head_dim ** -0.5)
    earlier = chosen_part[..., :, None] == chosen_part[..., None, :]
    before_slot = jnp.arange(picks)[:, None] > jnp.arange(picks)[None, :]
    repeated = jnp.any(earlier & before_slot[None, None], axis=-1)
    slot_open = jnp.repeat(jnp.logical_not(repeated), block_len, axis=-1)
    key_slot = jnp.arange(picks * block_len) // block_len
    key_place = jnp.arange(picks * block_len) % block_len
    query_place = jnp.arange(block_len)
    causal = (key_slot[None, :] > 0) | (key_place[None, :] <= query_place[:, None])
    visible = slot_open[:, :, None, None, :] & causal[None, None, None]
    highest = jnp.max(jnp.where(visible, scores, -jnp.inf), axis=-1, keepdims=True)
    weights = jnp.where(visible, jnp.exp(scores - highest), jnp.float32(0.0))
    totals = jnp.sum(weights, axis=-1)
    probabilities = lax.optimization_barrier(weights.astype(jnp.bfloat16)).astype(jnp.float32)
    attended = jnp.einsum("egaqk,egkh->gqeah", probabilities, value_part.astype(jnp.float32))
    scaled = attended / jnp.transpose(totals, (1, 3, 0, 2))[..., None]
    return scaled.astype(jnp.bfloat16)


def reference(queries, keys, values, chosen):
    tokens_all, query_heads, head_dim = queries.shape
    kv_heads = keys.shape[1]
    blocks = chosen.shape[1]
    picks = chosen.shape[2]
    block_len = tokens_all // blocks
    heads_per_group = query_heads // kv_heads
    group_size = 4

    def one_head(head_number):
        query_head = lax.dynamic_slice_in_dim(queries, head_number * heads_per_group, heads_per_group, 1)
        key_blocks = lax.dynamic_slice_in_dim(keys, head_number, 1, 1).reshape(blocks, block_len, head_dim)
        value_blocks = lax.dynamic_slice_in_dim(values, head_number, 1, 1).reshape(blocks, block_len, head_dim)
        chosen_head = lax.dynamic_index_in_dim(chosen, head_number, 0, keepdims=False)
        query_groups = query_head.reshape(blocks // group_size, group_size, block_len, 1, heads_per_group, head_dim)
        chosen_groups = chosen_head.reshape(blocks // group_size, group_size, picks)

        def block_group(operands):
            query_part, chosen_part = operands
            key_part = key_blocks[chosen_part].reshape(1, group_size, picks * block_len, head_dim)
            value_part = value_blocks[chosen_part].reshape(1, group_size, picks * block_len, head_dim)
            return attend(query_part, key_part, value_part, chosen_part[None])

        result = lax.map(block_group, (query_groups, chosen_groups))
        return result.reshape(tokens_all, heads_per_group, head_dim)

    stacked = lax.map(one_head, jnp.arange(kv_heads, dtype=jnp.int32))
    return jnp.transpose(stacked, (1, 0, 2, 3)).reshape(tokens_all, query_heads, head_dim)
```

```python
import math

import jax
import jax.numpy as jnp
from jax import lax
from jax.experimental import pallas as pl
from jax.experimental.pallas import tpu as pltpu
from jax.sharding import PartitionSpec as P

QUERY_HEADS = 32
KEY_VALUE_HEADS = 8
REMOTE_BLOCK_MAX = 2


NEGATIVE = -1e30


def attend_kernel(index_ref, plain_ref, open_ref, side_ref, q_ref, k_ref, v_ref, o_ref, ka, va):
    step = pl.program_id(0)
    blocks = pl.num_programs(0)
    rows_all, head_dim = q_ref.shape
    block_len = k_ref.shape[2]
    picks = ka.shape[0] // block_len
    side_rows = side_ref.shape[1]
    per_token = rows_all // block_len
    factor = head_dim ** -0.5 * math.log2(math.e)
    for s in range(picks):
        for h in range(2):
            place = index_ref[(h * blocks + step) * picks + s]
            at = (slice(s * block_len, (s + 1) * block_len), slice(h * head_dim, (h + 1) * head_dim))
            ka[at] = k_ref[h, place]
            va[at] = v_ref[h, place]

    def run(masked):
        for c in range(rows_all // side_rows):
            part = slice(c * side_rows, (c + 1) * side_rows)
            q = q_ref[part, :]
            qa = jnp.concatenate([q * side_ref[0], q * side_ref[1]], axis=1)
            row = lax.broadcasted_iota(jnp.int32, (side_rows, block_len), 0)
            lane = lax.broadcasted_iota(jnp.int32, (side_rows, block_len), 1)
            first = lax.rem(row, per_token) < per_token // 2
            token = lax.div(row, per_token) + c * (side_rows // per_token)
            scores = lax.dot_general(
                qa, ka[...], (((1,), (1,)), ((), ())), preferred_element_type=jnp.float32
            )
            parts = [scores[:, s * block_len : (s + 1) * block_len] for s in range(picks)]
            parts[0] = jnp.where(lane <= token, parts[0], NEGATIVE)
            if masked:
                for s in range(1, picks):
                    bias = [open_ref[(h * blocks + step) * picks + s] for h in range(2)]
                    bias = jnp.where(first, bias[0], bias[1])
                    parts[s] = jnp.where(bias > 0, parts[s], NEGATIVE)
            top = parts[0]
            for s in range(1, picks):
                top = jnp.maximum(top, parts[s])
            top = jnp.max(top, axis=1, keepdims=True)
            weights = [jnp.exp2((x - top) * factor) for x in parts]
            total = weights[0]
            for s in range(1, picks):
                total = total + weights[s]
            total = jnp.sum(total, axis=1, keepdims=True)
            probabilities = jnp.concatenate([w.astype(jnp.bfloat16) for w in weights], axis=1)
            out = jnp.dot(probabilities, va[...], preferred_element_type=jnp.float32)
            out = jnp.where(first, out[:, :head_dim], out[:, head_dim:])
            o_ref[part, :] = (out * (1.0 / total)).astype(o_ref.dtype)

    plain = plain_ref[step] > 0

    @pl.when(plain)
    def _():
        run(False)

    @pl.when(jnp.logical_not(plain))
    def _():
        run(True)


SIDE_ROWS = 256


def attend_all(queries, key_table, value_table, slot_index, slot_open):
    tokens_dev, query_heads, head_dim = queries.shape
    used_heads, table_blocks, block_len, _ = key_table.shape
    blocks, picks = slot_index.shape[1:]
    rows = block_len * query_heads
    flat = queries.reshape(tokens_dev * query_heads, head_dim)
    side = (jnp.arange(SIDE_ROWS) % query_heads < query_heads // 2)[None, :, None]
    side = jnp.concatenate([side, ~side], axis=0).astype(jnp.bfloat16)
    side = jnp.broadcast_to(side, (2, SIDE_ROWS, head_dim))
    whole = lambda shape: pl.BlockSpec(shape, lambda b, *_: (0,) * len(shape), pipeline_mode=pl.Buffered(1))
    plain = jnp.all(slot_open > 0, axis=(0, 2)).astype(jnp.int32)
    out = pl.pallas_call(
        attend_kernel,
        out_shape=jax.ShapeDtypeStruct(flat.shape, jnp.bfloat16),
        grid_spec=pltpu.PrefetchScalarGridSpec(
            num_scalar_prefetch=3,
            grid=(blocks,),
            in_specs=[
                whole(side.shape),
                pl.BlockSpec((rows, head_dim), lambda b, *_: (b, 0)),
                whole(key_table.shape),
                whole(value_table.shape),
            ],
            out_specs=pl.BlockSpec((rows, head_dim), lambda b, *_: (b, 0)),
            scratch_shapes=[
                pltpu.VMEM((picks * block_len, 2 * head_dim), jnp.bfloat16),
                pltpu.VMEM((picks * block_len, 2 * head_dim), jnp.bfloat16),
            ],
        ),
        compiler_params=pltpu.CompilerParams(
            dimension_semantics=("arbitrary",), vmem_limit_bytes=56 * 1024 * 1024
        ),
    )(slot_index.reshape(-1), plain, slot_open.reshape(-1), side, flat, key_table, value_table)
    return out.reshape(tokens_dev, query_heads, head_dim)


def on_device(queries, keys, values, chosen):
    tokens_dev, query_heads, head_dim = queries.shape
    blocks = chosen.shape[1]
    picks = chosen.shape[2]
    block_len = tokens_dev // blocks
    heads_per_group = QUERY_HEADS // KEY_VALUE_HEADS
    used_heads = max(1, query_heads // heads_per_group)
    per_head = query_heads // used_heads
    shard_count = lax.axis_size("ctx")
    position = lax.axis_index("ctx")
    rep_index = lax.axis_index("rep")
    first_head = rep_index * query_heads // heads_per_group
    chosen_used = lax.dynamic_slice_in_dim(chosen, first_head, used_heads, 0)
    fetch_keys = lax.dynamic_slice_in_dim(keys, first_head, used_heads, 1)
    fetch_values = lax.dynamic_slice_in_dim(values, first_head, used_heads, 1)
    fetch_heads = chosen_used.shape[0]
    flat_chosen = chosen_used.reshape(fetch_heads, blocks * picks)
    needed = jnp.any(
        flat_chosen[:, :, None] == jnp.arange(shard_count * blocks, dtype=jnp.int32)[None, None, :],
        axis=1,
    )
    needed = (
        needed.reshape(fetch_heads, shard_count, blocks)
        & (jnp.arange(shard_count, dtype=jnp.int32) != position)[None, :, None]
    )
    ranking = jnp.cumsum(needed.astype(jnp.int32), axis=2) - 1
    matches = needed[..., None] & (
        ranking[..., None] == jnp.arange(REMOTE_BLOCK_MAX, dtype=jnp.int32)[None, None, None, :]
    )
    request = jnp.sum(
        matches.astype(jnp.int32) * jnp.arange(blocks, dtype=jnp.int32)[None, None, :, None], axis=2
    )
    requests_in = lax.all_to_all(request, "ctx", split_axis=1, concat_axis=1, tiled=True)
    key_blocks = jnp.transpose(fetch_keys, (1, 0, 2)).reshape(
        fetch_heads, blocks, block_len, head_dim
    )
    value_blocks = jnp.transpose(fetch_values, (1, 0, 2)).reshape(
        fetch_heads, blocks, block_len, head_dim
    )
    fetch_index = jnp.arange(fetch_heads, dtype=jnp.int32)[:, None, None]
    send_keys = key_blocks[fetch_index, requests_in].reshape(
        fetch_heads, shard_count, REMOTE_BLOCK_MAX * block_len, head_dim
    )
    send_values = value_blocks[fetch_index, requests_in].reshape(
        fetch_heads, shard_count, REMOTE_BLOCK_MAX * block_len, head_dim
    )
    got_keys, got_values = (
        lax.all_to_all(send_keys, "ctx", split_axis=1, concat_axis=1, tiled=True),
        lax.all_to_all(send_values, "ctx", split_axis=1, concat_axis=1, tiled=True),
    )
    remote_keys = got_keys.reshape(used_heads, shard_count * REMOTE_BLOCK_MAX, block_len, head_dim)
    remote_values = got_values.reshape(
        used_heads, shard_count * REMOTE_BLOCK_MAX, block_len, head_dim
    )
    rank_used = ranking.reshape(used_heads, shard_count * blocks)
    key_table = jnp.concatenate([key_blocks, remote_keys], axis=1)
    value_table = jnp.concatenate([value_blocks, remote_values], axis=1)
    source = chosen_used // blocks
    within = chosen_used % blocks
    slot_rank = jnp.take_along_axis(
        rank_used, chosen_used.reshape(used_heads, blocks * picks), axis=1
    ).reshape(used_heads, blocks, picks)
    slot_index = jnp.where(
        source == position, within, blocks + source * REMOTE_BLOCK_MAX + slot_rank
    )
    before_slot = jnp.arange(picks)[:, None] > jnp.arange(picks)[None, :]
    same = chosen_used[..., :, None] == chosen_used[..., None, :]
    slot_open = jnp.logical_not(jnp.any(same & before_slot, axis=-1)).astype(jnp.int32)
    return attend_all(queries, key_table, value_table, slot_index, slot_open)


def solution(mesh):
    placed = (
        P(("groups", "ctx"), ("heads", "rep"), None),
        P(("groups", "ctx"), "heads", None),
        P(("groups", "ctx"), "heads", None),
        P("heads", ("groups", "ctx"), None),
    )
    return jax.shard_map(
        on_device,
        mesh=mesh,
        in_specs=placed,
        out_specs=P(("groups", "ctx"), ("heads", "rep"), None),
        check_vma=False,
    )
```

```python
import functools
import math

import jax
import jax.numpy as jnp
from jax import lax
from jax.experimental import pallas as pl
from jax.experimental.pallas import tpu as pltpu
from jax.sharding import PartitionSpec as P

QUERY_HEADS = 32
KEY_VALUE_HEADS = 8
REMOTE_BLOCK_MAX = 2
NEGATIVE = -1e30
BIG = 1 << 30
SIDE_ROWS = 256
PLAN_ROWS = 16
MESH = pl.DeviceIdType.MESH


def prepare_kernel(shards, query_heads, chosen_ref, k_hbm, v_hbm, *refs):
    plan_ref, kt_ref, vt_ref = refs[:3]
    send_refs = refs[3 : 3 + shards - 1]
    raw, ask, asked, asked_s, load_sem, send_sem, recv_sem, move_sem = refs[3 + shards - 1 :]
    me = lax.axis_index("ctx")
    heads, blocks, block_len, head_dim = kt_ref.shape
    first_head = lax.axis_index("rep") * query_heads // (QUERY_HEADS // KEY_VALUE_HEADS)
    kv_heads, picks, _ = chosen_ref.shape
    loads = [pltpu.make_async_copy(src, raw.at[i], load_sem.at[i]) for i, src in enumerate((k_hbm, v_hbm))]
    for load in loads:
        load.start()
    barrier = pltpu.get_barrier_semaphore()
    for d in range(1, shards):
        pl.semaphore_signal(barrier, inc=1, device_id={"ctx": lax.rem(me + d, shards)}, device_id_type=MESH)

    lane = lax.broadcasted_iota(jnp.int32, (8, 128), 1)
    tiles = [jnp.zeros((8, 128), jnp.int32) for _ in range(1, shards)]
    for h in range(heads):
        chosen = chosen_ref[first_head + h]
        base = me * blocks
        local = (chosen >= base) & (chosen < base + blocks)
        slot = jnp.where(local, chosen - base, 0)
        for d in range(1, shards):
            start = (me - d) * blocks
            inside = (chosen >= start) & (chosen < start + blocks)
            first = jnp.min(jnp.where(inside, chosen, BIG), keepdims=True)
            later = inside & (chosen > first)
            second = jnp.min(jnp.where(later, chosen, BIG), keepdims=True)
            slot = jnp.where(inside, blocks + (d - 1) * 2 * heads + later.astype(jnp.int32), slot)
            for r, place in enumerate((first, second)):
                place = jnp.clip(place - start, 0, blocks - 1)
                tiles[d - 1] = jnp.where(lane == h * 2 + r, place, tiles[d - 1])
        rows = [chosen[k : k + 1, :] for k in range(picks)]
        slots = [slot[k : k + 1, :] for k in range(picks)]
        near = [(x >= base) & (x < base + blocks) for x in rows]
        is_local, is_remote = [], []
        for k in range(picks):
            fresh = jnp.ones(rows[k].shape, jnp.int32)
            for j in range(k):
                fresh = jnp.where(rows[j] == rows[k], 0, fresh)
            is_local.append(jnp.where(near[k], fresh, 0))
            is_remote.append(jnp.where(near[k], 0, fresh))
        local_count = functools.reduce(jnp.add, is_local)
        place_of, at_local, at_remote = [], jnp.zeros_like(local_count), local_count
        for k in range(picks):
            place = jnp.where(is_local[k] > 0, at_local, at_remote)
            place_of.append(jnp.where(is_local[k] + is_remote[k] > 0, place, picks))
            at_local = at_local + is_local[k]
            at_remote = at_remote + is_remote[k]
        for p in range(picks):
            total = jnp.zeros_like(local_count)
            for k in range(picks):
                total = jnp.where(place_of[k] == p, slots[k], total)
            plan_ref[h * PLAN_ROWS + p : h * PLAN_ROWS + p + 1, :] = total
        plan_ref[h * PLAN_ROWS + picks : h * PLAN_ROWS + picks + 1, :] = local_count
        plan_ref[h * PLAN_ROWS + picks + 1 : h * PLAN_ROWS + picks + 2, :] = at_remote
        for p in range(picks + 2, PLAN_ROWS):
            plan_ref[h * PLAN_ROWS + p : h * PLAN_ROWS + p + 1, :] = jnp.zeros_like(local_count)
    for d in range(1, shards):
        ask[d - 1] = tiles[d - 1]
    pl.semaphore_wait(barrier, shards - 1)

    def request(d):
        return pltpu.make_async_remote_copy(
            src_ref=ask.at[d - 1],
            dst_ref=asked.at[d - 1],
            send_sem=send_sem.at[d - 1],
            recv_sem=recv_sem.at[d - 1],
            device_id={"ctx": lax.rem(me - d + shards, shards)},
            device_id_type=MESH,
        )

    for d in range(1, shards):

        @pl.when(me >= d)
        def _(d=d):
            request(d).start()

    for load in loads:
        load.wait()
    wide = kv_heads * block_len
    out_row = lax.broadcasted_iota(jnp.int32, (heads * block_len, wide), 0)
    in_row = lax.broadcasted_iota(jnp.int32, (heads * block_len, wide), 1)
    source = lax.rem(out_row, block_len) * kv_heads + first_head + lax.div(out_row, block_len)
    pick = jnp.where(source == in_row, 1.0, 0.0).astype(jnp.bfloat16)

    def split(b, carry):
        rows = pl.ds(pl.multiple_of(b * wide, wide), wide)
        for i, table in enumerate((kt_ref, vt_ref)):
            parted = jnp.dot(pick, raw[i, rows, :], preferred_element_type=jnp.float32).astype(jnp.bfloat16)
            for h in range(heads):
                table[h, b] = parted[h * block_len : (h + 1) * block_len, :]
        return carry

    lax.fori_loop(0, blocks, split, 0)
    for d in range(1, shards):

        @pl.when(me + d < shards)
        def _(d=d):
            request(d).wait_recv()
            move = pltpu.make_async_copy(asked.at[d - 1], asked_s.at[d - 1], move_sem.at[d - 1])
            move.start()
            move.wait()
            for h in range(heads):
                for r in range(2):
                    place = asked_s[d - 1, 0, h * 2 + r]
                    for i, table in enumerate((kt_ref, vt_ref)):
                        send_refs[d - 1][i, h * 2 + r] = table[h, place]

    for d in range(1, shards):

        @pl.when(me >= d)
        def _(d=d):
            request(d).wait_send()


def prepare(chosen, keys, values, shards, query_heads):
    kv_heads, picks, blocks = chosen.shape
    tokens, _, head_dim = keys.shape
    block_len = tokens // blocks
    heads = max(1, query_heads // (QUERY_HEADS // KEY_VALUE_HEADS))
    vmem = pl.BlockSpec(memory_space=pltpu.VMEM)
    table = jax.ShapeDtypeStruct((heads, blocks, block_len, head_dim), jnp.bfloat16)
    sent = jax.ShapeDtypeStruct((2, heads * 2, block_len, head_dim), jnp.bfloat16)
    partners = shards - 1
    return pl.pallas_call(
        functools.partial(prepare_kernel, shards, query_heads),
        out_shape=[jax.ShapeDtypeStruct((heads * PLAN_ROWS, blocks), jnp.int32), table, table] + [sent] * partners,
        in_specs=[vmem, pl.BlockSpec(memory_space=pl.ANY), pl.BlockSpec(memory_space=pl.ANY)],
        out_specs=[vmem] * (3 + partners),
        scratch_shapes=[
            pltpu.VMEM((2, tokens * kv_heads, head_dim), jnp.bfloat16),
            pltpu.VMEM((partners, 8, 128), jnp.int32),
            pltpu.VMEM((partners, 8, 128), jnp.int32),
            pltpu.SMEM((partners, 8, 128), jnp.int32),
            pltpu.SemaphoreType.DMA((2,)),
            pltpu.SemaphoreType.DMA((partners,)),
            pltpu.SemaphoreType.DMA((partners,)),
            pltpu.SemaphoreType.DMA((partners,)),
        ],
        compiler_params=pltpu.CompilerParams(
            collective_id=0, has_side_effects=True, vmem_limit_bytes=48 * 1024 * 1024
        ),
    )(chosen, keys.reshape(-1, head_dim), values.reshape(-1, head_dim))


def attend_step(heads, plan_ref, remote, picks, side_ref, q_ref, read, ka, va, finish):
    step = pl.program_id(0)
    rows_all, head_dim = q_ref.shape
    block_len = ka.shape[0] // picks
    per_token = rows_all // block_len
    shape = (SIDE_ROWS // 8, 8, head_dim)
    factor = head_dim ** -0.5 * math.log2(math.e)
    local = [plan_ref[h * PLAN_ROWS + picks, step] for h in range(heads)]
    every = [plan_ref[h * PLAN_ROWS + picks + 1, step] for h in range(heads)]
    start = local if remote else [0] * heads
    count = [every[h] - local[h] for h in range(heads)] if remote else local
    most = functools.reduce(jnp.maximum, count)

    def body(n):
        for s in range(n):
            for h in range(heads):
                spot = jnp.where(s < count[h], jnp.minimum(start[h] + s, picks - 1), start[h])
                spot = jnp.where(count[h] > 0, spot, 0)
                place = plan_ref[h * PLAN_ROWS + spot, step]
                at = (slice(s * block_len, (s + 1) * block_len), slice(h * head_dim, (h + 1) * head_dim))
                ka[at], va[at] = read(h, jnp.where(count[h] > 0, place, -1))
        low = lax.rem(lax.broadcasted_iota(jnp.int32, (1, 8, head_dim), 1), per_token) < per_token // 2
        bias = []
        for s in range(n):
            side_bias = [jnp.where(s < count[h], 0.0, NEGATIVE) for h in range(heads)]
            bias.append(jnp.where(low, side_bias[0], side_bias[-1]))
        row = lax.broadcasted_iota(jnp.int32, (SIDE_ROWS // 8, 8, block_len), 0)
        if per_token != 8:
            row = lax.div(row * 8 + lax.broadcasted_iota(jnp.int32, row.shape, 1), per_token)
        lane = lax.broadcasted_iota(jnp.int32, row.shape, 2)
        for c in range(rows_all // SIDE_ROWS):
            part = slice(c * SIDE_ROWS, (c + 1) * SIDE_ROWS)
            if n == 0:
                finish(part, None, None, None)
                continue
            q = q_ref[part, :]
            qa = q if heads == 1 else jnp.concatenate([q * side_ref[0], q * side_ref[1]], axis=1)
            scores = lax.dot_general(
                qa, ka[: n * block_len, :], (((1,), (1,)), ((), ())), preferred_element_type=jnp.float32
            )
            parts = [
                scores[:, s * block_len : (s + 1) * block_len].reshape(row.shape)
                for s in range(n)
            ]
            for s in range(n):
                if s == 0 and not remote:
                    parts[s] = jnp.where(lane <= row + c * (SIDE_ROWS // per_token), parts[s], NEGATIVE)
                else:
                    parts[s] = parts[s] + bias[s]
            top = functools.reduce(jnp.maximum, parts)
            top = jnp.max(top, axis=2, keepdims=True)
            weights = [jnp.exp2((x - top) * factor) for x in parts]
            total = jnp.sum(functools.reduce(jnp.add, weights), axis=2, keepdims=True)
            probabilities = jnp.concatenate(
                [w.reshape(SIDE_ROWS, block_len).astype(jnp.bfloat16) for w in weights], axis=1
            )
            out = jnp.dot(probabilities, va[: n * block_len, :], preferred_element_type=jnp.float32)
            if heads == 1:
                out = out.reshape(shape)
            else:
                out = jnp.where(low, out[:, :head_dim].reshape(shape), out[:, head_dim:].reshape(shape))
            finish(part, top, total, out)

    for n in range(0 if remote else 1, picks if remote else picks + 1):
        pl.when(most == n)(functools.partial(body, n))


def local_kernel(heads, picks, plan_ref, side_ref, q_ref, k_ref, v_ref, sum_ref, stat_ref, ka, va):
    head_dim = q_ref.shape[1]

    def read(h, place):
        place = jnp.maximum(place, 0)
        return k_ref[h, place], v_ref[h, place]

    def finish(part, top, total, out):
        half = lax.broadcasted_iota(jnp.int32, (1, 1, head_dim), 2) < head_dim // 2
        sum_ref[part, :] = out.reshape(-1, head_dim)
        stat_ref[part, :] = jnp.where(half, top, total).reshape(-1, head_dim)

    attend_step(heads, plan_ref, False, picks, side_ref, q_ref, read, ka, va, finish)


def remote_kernel(heads, picks, blocks, plan_ref, side_ref, q_ref, sum_ref, stat_ref, *refs):
    o_ref, table, ka, va, sem = refs[-5:]
    arrived = refs[:-5]
    rows_all, head_dim = q_ref.shape
    factor = head_dim ** -0.5 * math.log2(math.e)

    @pl.when(pl.program_id(0) == 0)
    def _():
        copies = [
            pltpu.make_async_copy(ref.at[i], table.at[i, pl.ds(2 * heads * d, 2 * heads)], sem.at[d, i])
            for d, ref in enumerate(arrived)
            for i in range(2)
        ]
        for copy in copies:
            copy.start()
        for copy in copies:
            copy.wait()

    def read(h, place):
        place = jnp.maximum(place - blocks, 0) + h * 2
        return table[0, place], table[1, place]

    def finish(part, top, total, out):
        shape = (-1, 8, head_dim)
        stat = stat_ref[part, :].reshape(shape)
        near_top, near_total = stat[:, :, :1], stat[:, :, head_dim - 1 :]
        near = sum_ref[part, :].reshape(shape)
        if top is not None:
            new_top = jnp.maximum(top, near_top)
            keep, add = jnp.exp2((near_top - new_top) * factor), jnp.exp2((top - new_top) * factor)
            near = near * keep + out * add
            near_total = near_total * keep + total * add
        near = near * (1.0 / near_total)
        o_ref[part, :] = near.reshape(-1, head_dim).astype(o_ref.dtype)

    attend_step(heads, plan_ref, True, picks, side_ref, q_ref, read, ka, va, finish)


def on_device(queries, keys, values, chosen):
    tokens_dev, query_heads, head_dim = queries.shape
    kv_heads, blocks, picks = chosen.shape
    block_len = tokens_dev // blocks
    shards = lax.axis_size("ctx")
    plan, key_table, value_table, *sent = prepare(jnp.transpose(chosen, (0, 2, 1)), keys, values, shards, query_heads)
    arrived = [
        lax.ppermute(block, "ctx", [(i, i + d) for i in range(shards - d)])
        for d, block in enumerate(sent, 1)
    ]
    rows = block_len * query_heads
    heads = key_table.shape[0]
    flat = queries.reshape(tokens_dev * query_heads, head_dim)
    side = (jnp.arange(SIDE_ROWS) % query_heads < query_heads // 2)[None, :, None]
    side = jnp.concatenate([side, ~side], axis=0).astype(jnp.bfloat16)
    side = jnp.broadcast_to(side, (2, SIDE_ROWS, head_dim))
    whole = lambda x: pl.BlockSpec(x.shape, lambda b, *_: (0,) * x.ndim, pipeline_mode=pl.Buffered(1))
    tile = pl.BlockSpec((rows, head_dim), lambda b, *_: (b, 0))
    pair = [pltpu.VMEM((picks * block_len, heads * head_dim), jnp.bfloat16)] * 2
    params = pltpu.CompilerParams(dimension_semantics=("arbitrary",), vmem_limit_bytes=48 * 1024 * 1024)
    cost = pl.CostEstimate(
        flops=4 * flat.size * picks * block_len, bytes_accessed=12 * flat.size, transcendentals=0
    )
    partial_sum, stat = pl.pallas_call(
        functools.partial(local_kernel, heads, picks),
        out_shape=[jax.ShapeDtypeStruct(flat.shape, jnp.float32)] * 2,
        grid_spec=pltpu.PrefetchScalarGridSpec(
            num_scalar_prefetch=1,
            grid=(blocks,),
            in_specs=[whole(side), tile, whole(key_table), whole(value_table)],
            out_specs=[tile, tile],
            scratch_shapes=pair,
        ),
        compiler_params=params,
        cost_estimate=cost,
    )(plan, side, flat, key_table, value_table)
    out = pl.pallas_call(
        functools.partial(remote_kernel, heads, picks, blocks),
        out_shape=jax.ShapeDtypeStruct(flat.shape, jnp.bfloat16),
        grid_spec=pltpu.PrefetchScalarGridSpec(
            num_scalar_prefetch=1,
            grid=(blocks,),
            in_specs=[whole(side), tile, tile, tile] + [pl.BlockSpec(memory_space=pl.ANY)] * len(arrived),
            out_specs=tile,
            scratch_shapes=[
                pltpu.VMEM((2, 2 * heads * len(arrived), block_len, head_dim), jnp.bfloat16),
                *pair,
                pltpu.SemaphoreType.DMA((len(arrived), 2)),
            ],
        ),
        compiler_params=params,
        cost_estimate=cost,
    )(plan, side, flat, partial_sum, stat, *arrived)
    return out.reshape(tokens_dev, query_heads, head_dim)


def solution(mesh):
    placed = (
        P(("groups", "ctx"), ("heads", "rep"), None),
        P(("groups", "ctx"), "heads", None),
        P(("groups", "ctx"), "heads", None),
        P("heads", ("groups", "ctx"), None),
    )
    return jax.shard_map(
        on_device,
        mesh=mesh,
        in_specs=placed,
        out_specs=P(("groups", "ctx"), ("heads", "rep"), None),
        check_vma=False,
    )
```

```python
import functools
import math

import jax
import jax.numpy as jnp
from jax import lax
from jax.experimental import pallas as pl
from jax.experimental.pallas import tpu as pltpu
from jax.sharding import PartitionSpec as P

QUERY_HEADS = 32
KEY_VALUE_HEADS = 8
REMOTE_BLOCK_MAX = 2
NEGATIVE = -1e30
BIG = 1 << 30
SIDE_ROWS = 256
PLAN_ROWS = 16
MESH = pl.DeviceIdType.MESH


def prepare_kernel(shards, query_heads, chosen_ref, k_hbm, v_hbm, *refs):
    plan_ref, kt_ref, vt_ref = refs[:3]
    send_refs = refs[3 : 3 + shards - 1]
    raw, ask, asked, asked_s, load_sem, send_sem, recv_sem, move_sem = refs[3 + shards - 1 :]
    me = lax.axis_index("ctx")
    heads, blocks, block_len, head_dim = kt_ref.shape
    first_head = lax.axis_index("rep") * query_heads // (QUERY_HEADS // KEY_VALUE_HEADS)
    kv_heads, picks, _ = chosen_ref.shape
    loads = [pltpu.make_async_copy(src, raw.at[i], load_sem.at[i]) for i, src in enumerate((k_hbm, v_hbm))]
    for load in loads:
        load.start()
    barrier = pltpu.get_barrier_semaphore()
    for d in range(1, shards):
        pl.semaphore_signal(barrier, inc=1, device_id={"ctx": lax.rem(me + d, shards)}, device_id_type=MESH)

    lane = lax.broadcasted_iota(jnp.int32, (8, 128), 1)
    tiles = [jnp.zeros((8, 128), jnp.int32) for _ in range(1, shards)]
    for h in range(heads):
        chosen = chosen_ref[first_head + h]
        base = me * blocks
        local = (chosen >= base) & (chosen < base + blocks)
        slot = jnp.where(local, chosen - base, 0)
        for d in range(1, shards):
            start = (me - d) * blocks
            inside = (chosen >= start) & (chosen < start + blocks)
            first = jnp.min(jnp.where(inside, chosen, BIG), keepdims=True)
            later = inside & (chosen > first)
            second = jnp.min(jnp.where(later, chosen, BIG), keepdims=True)
            slot = jnp.where(inside, blocks + (d - 1) * 2 * heads + later.astype(jnp.int32), slot)
            for r, place in enumerate((first, second)):
                place = jnp.clip(place - start, 0, blocks - 1)
                tiles[d - 1] = jnp.where(lane == h * 2 + r, place, tiles[d - 1])
        rows = [chosen[k : k + 1, :] for k in range(picks)]
        slots = [slot[k : k + 1, :] for k in range(picks)]
        near = [(x >= base) & (x < base + blocks) for x in rows]
        is_local, is_remote = [], []
        for k in range(picks):
            fresh = jnp.ones(rows[k].shape, jnp.int32)
            for j in range(k):
                fresh = jnp.where(rows[j] == rows[k], 0, fresh)
            is_local.append(jnp.where(near[k], fresh, 0))
            is_remote.append(jnp.where(near[k], 0, fresh))
        local_count = functools.reduce(jnp.add, is_local)
        place_of, at_local, at_remote = [], jnp.zeros_like(local_count), local_count
        for k in range(picks):
            place = jnp.where(is_local[k] > 0, at_local, at_remote)
            place_of.append(jnp.where(is_local[k] + is_remote[k] > 0, place, picks))
            at_local = at_local + is_local[k]
            at_remote = at_remote + is_remote[k]
        for p in range(picks):
            total = jnp.zeros_like(local_count)
            for k in range(picks):
                total = jnp.where(place_of[k] == p, slots[k], total)
            plan_ref[h * PLAN_ROWS + p : h * PLAN_ROWS + p + 1, :] = total
        plan_ref[h * PLAN_ROWS + picks : h * PLAN_ROWS + picks + 1, :] = local_count
        plan_ref[h * PLAN_ROWS + picks + 1 : h * PLAN_ROWS + picks + 2, :] = at_remote
        for p in range(picks + 2, PLAN_ROWS):
            plan_ref[h * PLAN_ROWS + p : h * PLAN_ROWS + p + 1, :] = jnp.zeros_like(local_count)
    for d in range(1, shards):
        ask[d - 1] = tiles[d - 1]
    pl.semaphore_wait(barrier, shards - 1)

    def request(d):
        return pltpu.make_async_remote_copy(
            src_ref=ask.at[d - 1],
            dst_ref=asked.at[d - 1],
            send_sem=send_sem.at[d - 1],
            recv_sem=recv_sem.at[d - 1],
            device_id={"ctx": lax.rem(me - d + shards, shards)},
            device_id_type=MESH,
        )

    for d in range(1, shards):

        @pl.when(me >= d)
        def _(d=d):
            request(d).start()

    for load in loads:
        load.wait()
    wide = kv_heads * block_len
    out_row = lax.broadcasted_iota(jnp.int32, (heads * block_len, wide), 0)
    in_row = lax.broadcasted_iota(jnp.int32, (heads * block_len, wide), 1)
    source = lax.rem(out_row, block_len) * kv_heads + first_head + lax.div(out_row, block_len)
    pick = jnp.where(source == in_row, 1.0, 0.0).astype(jnp.bfloat16)

    def split(b, carry):
        rows = pl.ds(pl.multiple_of(b * wide, wide), wide)
        for i, table in enumerate((kt_ref, vt_ref)):
            parted = jnp.dot(pick, raw[i, rows, :], preferred_element_type=jnp.float32).astype(jnp.bfloat16)
            for h in range(heads):
                table[h, b] = parted[h * block_len : (h + 1) * block_len, :]
        return carry

    lax.fori_loop(0, blocks, split, 0)
    for d in range(1, shards):

        @pl.when(me + d < shards)
        def _(d=d):
            request(d).wait_recv()
            move = pltpu.make_async_copy(asked.at[d - 1], asked_s.at[d - 1], move_sem.at[d - 1])
            move.start()
            move.wait()
            for h in range(heads):
                for r in range(2):
                    place = asked_s[d - 1, 0, h * 2 + r]
                    for i, table in enumerate((kt_ref, vt_ref)):
                        send_refs[d - 1][i, h * 2 + r] = table[h, place]

    for d in range(1, shards):

        @pl.when(me >= d)
        def _(d=d):
            request(d).wait_send()


def prepare(chosen, keys, values, shards, query_heads):
    kv_heads, picks, blocks = chosen.shape
    tokens, _, head_dim = keys.shape
    block_len = tokens // blocks
    heads = max(1, query_heads // (QUERY_HEADS // KEY_VALUE_HEADS))
    vmem = pl.BlockSpec(memory_space=pltpu.VMEM)
    table = jax.ShapeDtypeStruct((heads, blocks, block_len, head_dim), jnp.bfloat16)
    sent = jax.ShapeDtypeStruct((2, heads * 2, block_len, head_dim), jnp.bfloat16)
    partners = shards - 1
    return pl.pallas_call(
        functools.partial(prepare_kernel, shards, query_heads),
        out_shape=[jax.ShapeDtypeStruct((heads * PLAN_ROWS, blocks), jnp.int32), table, table] + [sent] * partners,
        in_specs=[vmem, pl.BlockSpec(memory_space=pl.ANY), pl.BlockSpec(memory_space=pl.ANY)],
        out_specs=[vmem] * (3 + partners),
        scratch_shapes=[
            pltpu.VMEM((2, tokens * kv_heads, head_dim), jnp.bfloat16),
            pltpu.VMEM((partners, 8, 128), jnp.int32),
            pltpu.VMEM((partners, 8, 128), jnp.int32),
            pltpu.SMEM((partners, 8, 128), jnp.int32),
            pltpu.SemaphoreType.DMA((2,)),
            pltpu.SemaphoreType.DMA((partners,)),
            pltpu.SemaphoreType.DMA((partners,)),
            pltpu.SemaphoreType.DMA((partners,)),
        ],
        compiler_params=pltpu.CompilerParams(
            collective_id=0, has_side_effects=True, vmem_limit_bytes=48 * 1024 * 1024
        ),
    )(chosen, keys.reshape(-1, head_dim), values.reshape(-1, head_dim))


def attend_step(heads, plan_ref, remote, picks, side_ref, q_ref, read, ka, va, finish):
    step = pl.program_id(0)
    rows_all, head_dim = q_ref.shape
    block_len = ka.shape[0] // picks
    per_token = rows_all // block_len
    shape = (SIDE_ROWS // 8, 8, head_dim)
    factor = head_dim ** -0.5 * math.log2(math.e)
    local = [plan_ref[h * PLAN_ROWS + picks, step] for h in range(heads)]
    every = [plan_ref[h * PLAN_ROWS + picks + 1, step] for h in range(heads)]
    start = local if remote else [0] * heads
    count = [every[h] - local[h] for h in range(heads)] if remote else local
    most = functools.reduce(jnp.maximum, count)

    def body(n):
        for s in range(n):
            for h in range(heads):
                spot = jnp.where(s < count[h], jnp.minimum(start[h] + s, picks - 1), start[h])
                spot = jnp.where(count[h] > 0, spot, 0)
                place = plan_ref[h * PLAN_ROWS + spot, step]
                at = (slice(s * block_len, (s + 1) * block_len), slice(h * head_dim, (h + 1) * head_dim))
                ka[at], va[at] = read(h, jnp.where(count[h] > 0, place, -1))
        low = lax.rem(lax.broadcasted_iota(jnp.int32, (1, 8, head_dim), 1), per_token) < per_token // 2
        bias = []
        for s in range(n):
            side_bias = [jnp.where(s < count[h], 0.0, NEGATIVE) for h in range(heads)]
            bias.append(jnp.where(low, side_bias[0], side_bias[-1]))
        row = lax.broadcasted_iota(jnp.int32, (SIDE_ROWS // 8, 8, block_len), 0)
        if per_token != 8:
            row = lax.div(row * 8 + lax.broadcasted_iota(jnp.int32, row.shape, 1), per_token)
        lane = lax.broadcasted_iota(jnp.int32, row.shape, 2)
        for c in range(rows_all // SIDE_ROWS):
            part = slice(c * SIDE_ROWS, (c + 1) * SIDE_ROWS)
            if n == 0:
                finish(part, None, None, None)
                continue
            q = q_ref[part, :]
            qa = q if heads == 1 else jnp.concatenate([q * side_ref[0], q * side_ref[1]], axis=1)
            scores = lax.dot_general(
                qa, ka[: n * block_len, :], (((1,), (1,)), ((), ())), preferred_element_type=jnp.float32
            )
            parts = [
                scores[:, s * block_len : (s + 1) * block_len].reshape(row.shape)
                for s in range(n)
            ]
            for s in range(n):
                if s == 0 and not remote:
                    parts[s] = jnp.where(lane <= row + c * (SIDE_ROWS // per_token), parts[s], NEGATIVE)
                else:
                    parts[s] = parts[s] + bias[s]
            top = functools.reduce(jnp.maximum, parts)
            top = jnp.max(top, axis=2, keepdims=True)
            weights = [jnp.exp2((x - top) * factor) for x in parts]
            total = jnp.sum(functools.reduce(jnp.add, weights), axis=2, keepdims=True)
            probabilities = jnp.concatenate(
                [w.reshape(SIDE_ROWS, block_len).astype(jnp.bfloat16) for w in weights], axis=1
            )
            out = jnp.dot(probabilities, va[: n * block_len, :], preferred_element_type=jnp.float32)
            if heads == 1:
                out = out.reshape(shape)
            else:
                out = jnp.where(low, out[:, :head_dim].reshape(shape), out[:, head_dim:].reshape(shape))
            finish(part, top, total, out)

    for n in range(0 if remote else 1, picks if remote else picks + 1):
        pl.when(most == n)(functools.partial(body, n))


def local_kernel(heads, picks, plan_ref, side_ref, q_ref, k_ref, v_ref, sum_ref, top_ref, total_ref, ka, va):
    head_dim = q_ref.shape[1]

    def read(h, place):
        place = jnp.maximum(place, 0)
        return k_ref[h, place], v_ref[h, place]

    def finish(part, top, total, out):
        sum_ref[part, :] = out.reshape(-1, head_dim)
        top_ref[part, :] = jnp.broadcast_to(top, out.shape).reshape(-1, head_dim)
        total_ref[part, :] = jnp.broadcast_to(total, out.shape).reshape(-1, head_dim)

    attend_step(heads, plan_ref, False, picks, side_ref, q_ref, read, ka, va, finish)


def remote_kernel(heads, picks, blocks, plan_ref, side_ref, q_ref, sum_ref, top_ref, total_ref, *refs):
    o_ref, table, ka, va, sem = refs[-5:]
    arrived = refs[:-5]
    rows_all, head_dim = q_ref.shape
    factor = head_dim ** -0.5 * math.log2(math.e)

    @pl.when(pl.program_id(0) == 0)
    def _():
        copies = [
            pltpu.make_async_copy(ref.at[i], table.at[i, pl.ds(2 * heads * d, 2 * heads)], sem.at[d, i])
            for d, ref in enumerate(arrived)
            for i in range(2)
        ]
        for copy in copies:
            copy.start()
        for copy in copies:
            copy.wait()

    def read(h, place):
        place = jnp.maximum(place - blocks, 0) + h * 2
        return table[0, place], table[1, place]

    def finish(part, top, total, out):
        shape = (-1, 8, head_dim)
        near_top, near_total = top_ref[part, :].reshape(shape), total_ref[part, :].reshape(shape)
        near = sum_ref[part, :].reshape(shape)
        if top is not None:
            new_top = jnp.maximum(top, near_top)
            keep, add = jnp.exp2((near_top - new_top) * factor), jnp.exp2((top - new_top) * factor)
            near = near * keep + out * add
            near_total = near_total * keep + total * add
        near = near * (1.0 / near_total)
        o_ref[part, :] = near.reshape(-1, head_dim).astype(o_ref.dtype)

    attend_step(heads, plan_ref, True, picks, side_ref, q_ref, read, ka, va, finish)


def on_device(queries, keys, values, chosen):
    tokens_dev, query_heads, head_dim = queries.shape
    kv_heads, blocks, picks = chosen.shape
    block_len = tokens_dev // blocks
    shards = lax.axis_size("ctx")
    plan, key_table, value_table, *sent = prepare(jnp.transpose(chosen, (0, 2, 1)), keys, values, shards, query_heads)
    arrived = [
        lax.ppermute(block, "ctx", [(i, i + d) for i in range(shards - d)])
        for d, block in enumerate(sent, 1)
    ]
    rows = block_len * query_heads
    heads = key_table.shape[0]
    flat = queries.reshape(tokens_dev * query_heads, head_dim)
    side = (jnp.arange(SIDE_ROWS) % query_heads < query_heads // 2)[None, :, None]
    side = jnp.concatenate([side, ~side], axis=0).astype(jnp.bfloat16)
    side = jnp.broadcast_to(side, (2, SIDE_ROWS, head_dim))
    whole = lambda x: pl.BlockSpec(x.shape, lambda b, *_: (0,) * x.ndim, pipeline_mode=pl.Buffered(1))
    tile = pl.BlockSpec((rows, head_dim), lambda b, *_: (b, 0))
    pair = [pltpu.VMEM((picks * block_len, heads * head_dim), jnp.bfloat16)] * 2
    params = pltpu.CompilerParams(dimension_semantics=("arbitrary",), vmem_limit_bytes=48 * 1024 * 1024)
    cost = pl.CostEstimate(
        flops=4 * flat.size * picks * block_len, bytes_accessed=12 * flat.size, transcendentals=0
    )
    partials = pl.pallas_call(
        functools.partial(local_kernel, heads, picks),
        out_shape=[jax.ShapeDtypeStruct(flat.shape, jnp.float32)] * 3,
        grid_spec=pltpu.PrefetchScalarGridSpec(
            num_scalar_prefetch=1,
            grid=(blocks,),
            in_specs=[whole(side), tile, whole(key_table), whole(value_table)],
            out_specs=[tile] * 3,
            scratch_shapes=pair,
        ),
        compiler_params=params,
        cost_estimate=cost,
    )(plan, side, flat, key_table, value_table)
    out = pl.pallas_call(
        functools.partial(remote_kernel, heads, picks, blocks),
        out_shape=jax.ShapeDtypeStruct(flat.shape, jnp.bfloat16),
        grid_spec=pltpu.PrefetchScalarGridSpec(
            num_scalar_prefetch=1,
            grid=(blocks,),
            in_specs=[whole(side), tile, tile, tile, tile] + [pl.BlockSpec(memory_space=pl.ANY)] * len(arrived),
            out_specs=tile,
            scratch_shapes=[
                pltpu.VMEM((2, 2 * heads * len(arrived), block_len, head_dim), jnp.bfloat16),
                *pair,
                pltpu.SemaphoreType.DMA((len(arrived), 2)),
            ],
        ),
        compiler_params=params,
        cost_estimate=cost,
    )(plan, side, flat, *partials, *arrived)
    return out.reshape(tokens_dev, query_heads, head_dim)


def solution(mesh):
    placed = (
        P(("groups", "ctx"), ("heads", "rep"), None),
        P(("groups", "ctx"), "heads", None),
        P(("groups", "ctx"), "heads", None),
        P("heads", ("groups", "ctx"), None),
    )
    return jax.shard_map(
        on_device,
        mesh=mesh,
        in_specs=placed,
        out_specs=P(("groups", "ctx"), ("heads", "rep"), None),
        check_vma=False,
    )
```
